1024 devices in a mesh: row: 16 (over y, x), col: 64 (over z, core).
Axes of the slice: x: 4, y: 4, z: 32, core: 2. Of those that a mesh axis runs over, the one named last changes fastest.
Arguments:
- spectra: float32 [16384, 8192], P('row', 'col'), may hold values from 0.15 to 16.61, as said below
- factor_w: float32 [16384, 128], P('row'), may hold values from 0.035 to 3.6, as said below
- factor_h: float32 [128, 8192], P(None, 'col'), may hold values from 0.035 to 3.6, as said below
Outputs:
- final_w: float32 [16384, 128], P('row')
- final_h: float32 [128, 8192], P(None, 'col')
The draws below stay inside these ranges and needn't reach their ends.
Inputs may be any that keep to these rules, and one draw needn't show every extreme that they name: `spectra`: strictly positive entries. `factor_w`: strictly positive entries. `factor_h`: strictly positive entries.
All inputs are finite; a program needn't handle non-finite values.
Results may differ from the reference program's by a relative error of at most 0.00011.
Values sent between devices are 32-bit elements; how exact they have to be, the bound alone decides.
A program may use at most 32 MiB of HBM per device.

```python
import jax
import jax.numpy as jnp
from jax import lax

RANK = 128
SPECTRA = 16384
PIXELS = 8192


def jitter_of(key, shape):
    return jnp.exp(jax.random.uniform(key, shape, jnp.float32, jnp.log(0.7), 0.0))


def draw_spectra(key, part):
    rows = jnp.arange(SPECTRA, dtype=jnp.int32)
    block = rows * RANK // SPECTRA
    table = jax.random.uniform(jax.random.fold_in(key, 31), (RANK, PIXELS), jnp.float32, -1.2, 1.2)
    lift = jnp.exp(table[block])
    base_key = jax.random.fold_in(key, 32)
    base = jnp.exp(jax.random.uniform(base_key, (SPECTRA, PIXELS), jnp.float32, jnp.log(0.5), jnp.log(5.0)))
    return base * lift


def draw_factor_w(key, part):
    rows = jnp.arange(SPECTRA, dtype=jnp.int32)
    block = rows * RANK // SPECTRA
    owner = jax.random.permutation(jax.random.fold_in(key, 11), RANK)[block]
    owned = owner[:, None] == jnp.arange(RANK, dtype=jnp.int32)[None, :]
    ramp = 1.0 + 2.0 * rows.astype(jnp.float32)[:, None] / max(SPECTRA - 1, 1)
    level = jnp.where(owned, jnp.float32(3.6), 0.05 * ramp)
    return level * jitter_of(jax.random.fold_in(key, 12), (SPECTRA, RANK))


def draw_factor_h(key, part):
    cols = jnp.arange(PIXELS, dtype=jnp.int32)
    block = cols * RANK // PIXELS
    owner = jax.random.permutation(jax.random.fold_in(key, 21), RANK)[block]
    owned = jnp.arange(RANK, dtype=jnp.int32)[:, None] == owner[None, :]
    ramp = 1.0 + 2.0 * cols.astype(jnp.float32)[None, :] / max(PIXELS - 1, 1)
    level = jnp.where(owned, jnp.float32(3.6), 0.05 * ramp)
    return level * jitter_of(jax.random.fold_in(key, 22), (RANK, PIXELS))


def setup_inputs(seed: int = 0) -> dict:
    keys = jax.random.split(jax.random.key(seed), 4)
    spectra = draw_spectra(jax.random.fold_in(keys[3], 71), 0)
    factor_w = draw_factor_w(jax.random.fold_in(keys[3], 71), 0)
    factor_h = draw_factor_h(jax.random.fold_in(keys[3], 71), 0)
    return dict(spectra=spectra, factor_w=factor_w, factor_h=factor_h)


def ratio_of(spectra, w_fac, h_fac):
    approx = jnp.dot(w_fac, h_fac, preferred_element_type=jnp.float32, precision=lax.Precision.HIGHEST)
    return spectra / approx


def update_h(spectra, w_fac, h_fac):
    ratio = ratio_of(spectra, w_fac, h_fac)
    numer = lax.dot_general(w_fac, ratio, (((0,), (0,)), ((), ())), precision=lax.Precision.HIGHEST, preferred_element_type=jnp.float32)
    colsum = jnp.sum(w_fac, axis=0)
    return h_fac * numer / colsum[:, None]


def update_w(spectra, w_fac, h_fac):
    ratio = ratio_of(spectra, w_fac, h_fac)
    numer = lax.dot_general(ratio, h_fac, (((1,), (1,)), ((), ())), precision=lax.Precision.HIGHEST, preferred_element_type=jnp.float32)
    rowsum = jnp.sum(h_fac, axis=1)
    return w_fac * numer / rowsum[None, :]


def reference(spectra, factor_w, factor_h):
    w_fac, h_fac = factor_w, factor_h
    for which in range(3):
        h_fac = update_h(spectra, w_fac, h_fac)
    w_fac = update_w(spectra, w_fac, h_fac)
    for which in range(2):
        h_fac = update_h(spectra, w_fac, h_fac)
    return w_fac, h_fac
```

```python
import functools

import jax
import jax.numpy as jnp
from jax import lax
from jax.experimental import pallas as pl
from jax.experimental.pallas import tpu as pltpu
from jax.sharding import PartitionSpec as P

MESH = pl.DeviceIdType.MESH
F32 = jnp.float32
BF16 = jnp.bfloat16
HALF = 64
EXTRA = 8
BLOCK = HALF + EXTRA
CHUNK = 256


def two_terms(x):
    hi = x.astype(BF16)
    lo = (x - hi.astype(F32)).astype(BF16)
    return hi, lo


def twice(x):
    hi, lo = two_terms(x)
    row = jnp.concatenate([hi, lo], axis=1)
    return jnp.concatenate([row, row], axis=0)


def dot(a, b):
    return jnp.dot(a, b, preferred_element_type=F32)


def folded(x):
    return x.reshape(-1, 8, x.shape[-1]).sum(axis=0)


def kernel(
    v_ref, w_in, h_in, w_out, h_out,
    h_ref, wcat, wtcat, hcat, rcat, cpart, numer,
    xb, x_send, x_recv,
    nw, pair, red, win, tot,
    p_send, p_recv, n_send, n_recv, s_send, s_recv, g_send, g_recv, q_send, q_recv,
):
    row = lax.axis_index("row")
    col = lax.axis_index("col")
    y, x = row // 4, row % 4
    z, core = col // 2, col % 2
    other = 1 - core
    kind, group = z % 8, z // 8

    def along_x(d):
        return (y * 4 + (x + d) % 4, col)

    def along_y(d):
        return (((y + d) % 4) * 4 + x, col)

    def along_z(d):
        return (row, ((z + d + 32) % 32) * 2 + core)

    partner = (row, z * 2 + other)
    window = (4, -4, 3, -3, 2, -2, 1, -1)
    strides = (16, 8, 24)
    peers = [along_x(d) for d in (1, 2, 3)] + [along_y(d) for d in (1, 2, 3)]
    peers += [partner] + [along_z(d) for d in window] + [along_z(d) for d in strides]

    barrier = pltpu.get_barrier_semaphore()
    for p in peers:
        pl.semaphore_signal(barrier, inc=1, device_id=p, device_id_type=MESH)

    def take_w(src):
        for b in range(8):
            rows = pl.ds(b * 128, 128)
            w = src[rows, :]
            hi, lo = two_terms(w)
            wcat[rows, 0:128] = hi
            wcat[rows, 128:256] = lo
            hi, lo = two_terms(w.T)
            wtcat[0:128, rows] = hi
            wtcat[128:256, rows] = lo
        cpart[...] = folded(src[...])

    def ratio_block(b):
        rows = pl.ds(b * CHUNK, CHUNK)
        both = dot(wcat[rows, :], hcat[...])
        ratio = v_ref[rows, :] / (both[:, 0:128] + both[:, 128:256])
        hi, lo = two_terms(ratio)
        return jnp.concatenate([hi, lo], axis=1)

    def local_numer():
        acc = jnp.zeros((256, 256), F32)
        for b in range(1024 // CHUNK):
            acc += dot(wtcat[:, b * CHUNK : (b + 1) * CHUNK], ratio_block(b))
        low = acc[128:256, 0:128] + acc[0:128, 128:256] + acc[128:256, 128:256]
        return acc[0:128, 0:128] + low

    mine = (x, y)
    ring = (along_x, along_y)

    def copies(slot, phase, half):
        axis = half if phase == 0 else 1 - half
        me = mine[axis]
        size = BLOCK if half == 0 else HALF
        out, into = [], []
        for d in (2, 1, 3):
            for at, got in ((me, out), ((me + d) % 4, into)):
                block = xb.at[slot, phase, half, at, pl.ds(0, size)]
                got.append(
                    pltpu.make_async_remote_copy(
                        src_ref=block,
                        dst_ref=block,
                        send_sem=x_send.at[slot, phase, half, d - 1],
                        recv_sem=x_recv.at[slot, phase, half, at],
                        device_id=ring[axis](d),
                        device_id_type=MESH,
                    )
                )
        return me, size, out, into

    def total_of(slot, phase, half, size):
        parts = [xb[slot, phase, half, i, 0:size] for i in range(4)]
        return (parts[0] + parts[1]) + (parts[2] + parts[3])

    def update_h(slot, entry=None):
        new = local_numer()
        plans = [[copies(slot, phase, half) for half in (0, 1)] for phase in (0, 1)]
        xb[slot, 0, 0, x, 0:HALF] = new[0:HALF]
        xb[slot, 0, 0, x, HALF:BLOCK] = cpart[...]
        xb[slot, 0, 1, y, 0:HALF] = new[HALF : 2 * HALF]
        if entry is not None:
            entry()
        for half in (0, 1):
            for c in plans[0][half][2]:
                c.start()
        for half in (0, 1):
            _, size, _, into = plans[0][half]
            for c in into:
                c.wait_recv()
            xb[slot, 1, half, plans[1][half][0], 0:size] = total_of(slot, 0, half, size)
            for c in plans[1][half][2]:
                c.start()
        for half in (0, 1):
            for c in plans[1][half][3]:
                c.wait_recv()
        top = total_of(slot, 1, 0, BLOCK)
        colsum = jnp.sum(top[HALF:BLOCK], axis=0, keepdims=True)
        over = jnp.broadcast_to(colsum, (128, 128)).T
        full = jnp.concatenate([top[0:HALF], total_of(slot, 1, 1, HALF)], axis=0)
        fresh = h_ref[...] * full / over
        h_ref[...] = fresh
        hcat[...] = twice(fresh)
        for phase in (0, 1):
            for half in (0, 1):
                for c in plans[phase][half][2]:
                    c.wait_send()

    def remote(src, dst, send, recv, to):
        return pltpu.make_async_remote_copy(
            src_ref=src, dst_ref=dst, send_sem=send, recv_sem=recv, device_id=to, device_id_type=MESH
        )

    def update_w():
        turned = h_ref[...].T
        weights = twice(turned)
        for b in range(1024 // CHUNK):
            both = dot(ratio_block(b), weights)
            both = both[:, 0:128] + both[:, 128:256]
            for i in range(CHUNK // HALF):
                nw[b * (CHUNK // HALF) + i] = both[i * HALF : (i + 1) * HALF]
        rowsum = folded(turned)
        nw[16, 0:EXTRA] = rowsum
        give = [
            remote(nw.at[pl.ds(other * 8, 8)], pair.at[pl.ds(0, 8)], p_send.at[0], p_recv.at[0], partner),
            remote(nw.at[16, pl.ds(0, EXTRA)], pair.at[8, pl.ds(0, EXTRA)], p_send.at[1], p_recv.at[1], partner),
        ]
        for c in give:
            c.start()
        for c in give:
            c.wait_recv()
        both_rows = rowsum + pair[8, 0:EXTRA]
        for k in range(8):
            red[k, 0:EXTRA] = both_rows
            red[k, EXTRA:BLOCK] = nw[core * 8 + k] + pair[k]
        middle = EXTRA + HALF // 2

        def spans(d):
            if d == 4:
                return 0, middle
            if d == -4:
                return middle, BLOCK - middle
            return 0, BLOCK

        scatter = []
        for i, d in enumerate(window):
            a, n = spans(d)
            place = min(i, 7) if d != -4 else 0
            scatter.append(
                remote(
                    red.at[(kind + d + 8) % 8, pl.ds(a, n)],
                    win.at[place, pl.ds(a, n)],
                    n_send.at[i],
                    n_recv.at[i],
                    along_z(d),
                )
            )
        for c in scatter:
            c.start()
        for c in scatter:
            c.wait_recv()
        acc = red[kind] + win[0]
        for i in range(2, 8):
            acc += win[i]
        tot[group] = acc
        share = []
        for i, d in enumerate(strides):
            share.append(
                remote(tot.at[group], tot.at[group], s_send.at[i], s_recv.at[group], along_z(d))
            )
        for c in share:
            c.start()
        for i, d in enumerate(strides):
            at = (group + d // 8) % 4
            remote(tot.at[at], tot.at[at], s_send.at[i], s_recv.at[at], along_z(d)).wait_recv()
        full = (tot[0] + tot[1]) + (tot[2] + tot[3])
        below = jnp.sum(full[0:EXTRA], axis=0, keepdims=True)
        here = pl.ds(pl.multiple_of(core * 512 + kind * HALF, HALF), HALF)
        w_out[here, :] = w_in[here, :] * full[EXTRA:BLOCK] / below

        def part(which, owner, d):
            base = which * 512 + owner * HALF
            a, n = (0, HALF // 2) if d == 4 else (HALF // 2, HALF // 2) if d == -4 else (0, HALF)
            return w_out.at[pl.ds(pl.multiple_of(base + a, HALF // 2), n), :]

        spread = []
        for i, d in enumerate(window):
            block = part(core, kind, d)
            spread.append(remote(block, block, g_send.at[i], g_recv.at[i], along_z(d)))
        for c in spread:
            c.start()
        mine_now = part(core, kind, 0)
        over = [remote(mine_now, mine_now, q_send.at[8], q_recv.at[8], partner)]
        over[0].start()
        for i, d in enumerate(window):
            spread[i].wait_recv()
            owner = (kind - d + 8) % 8
            block = part(core, owner, d)
            c = remote(block, block, q_send.at[i], q_recv.at[i], partner)
            c.start()
            over.append(c)
        for c in over:
            c.wait_recv()
        for c in give + scatter + share + spread + over:
            c.wait_send()

    take_w(w_in)
    h_ref[...] = h_in[...]
    hcat[...] = twice(h_in[...])
    update_h(0, lambda: pl.semaphore_wait(barrier, len(peers)))
    update_h(1)
    update_h(0)
    update_w()
    take_w(w_out)
    update_h(1)
    update_h(0)
    h_out[...] = h_ref[...]


def per_device(spectra, factor_w, factor_h):
    vmem = pl.BlockSpec(memory_space=pltpu.VMEM)
    dma = pltpu.SemaphoreType.DMA
    return pl.pallas_call(
        kernel,
        out_shape=(
            jax.ShapeDtypeStruct((1024, 128), F32),
            jax.ShapeDtypeStruct((128, 128), F32),
        ),
        in_specs=[vmem] * 3,
        out_specs=(vmem, vmem),
        scratch_shapes=[
            pltpu.VMEM((128, 128), F32),
            pltpu.VMEM((1024, 256), BF16),
            pltpu.VMEM((256, 1024), BF16),
            pltpu.VMEM((256, 256), BF16),
            pltpu.VMEM((1024, 256), BF16),
            pltpu.VMEM((EXTRA, 128), F32),
            pltpu.VMEM((128, 128), F32),
            pltpu.VMEM((2, 2, 2, 4, BLOCK, 128), F32),
            dma((2, 2, 2, 3)),
            dma((2, 2, 2, 4)),
            pltpu.VMEM((17, HALF, 128), F32),
            pltpu.VMEM((9, HALF, 128), F32),
            pltpu.VMEM((8, BLOCK, 128), F32),
            pltpu.VMEM((8, BLOCK, 128), F32),
            pltpu.VMEM((4, BLOCK, 128), F32),
            dma((2,)), dma((2,)),
            dma((8,)), dma((8,)),
            dma((3,)), dma((4,)),
            dma((8,)), dma((8,)),
            dma((9,)), dma((9,)),
        ],
        compiler_params=pltpu.CompilerParams(collective_id=0, has_side_effects=True),
        name="nmf",
    )(spectra, factor_w, factor_h)


def solution(mesh):
    return jax.shard_map(
        per_device,
        mesh=mesh,
        in_specs=(P("row", "col"), P("row", None), P(None, "col")),
        out_specs=(P("row", None), P(None, "col")),
        check_vma=False,
    )
```

```python
import functools

import jax
import jax.numpy as jnp
from jax import lax
from jax.experimental import pallas as pl
from jax.experimental.pallas import tpu as pltpu
from jax.sharding import PartitionSpec as P

MESH = pl.DeviceIdType.MESH
F32 = jnp.float32
BF16 = jnp.bfloat16
HALF = 64
EXTRA = 8
BLOCK = HALF + EXTRA
CHUNK = 256
PARTS = 2
PART = HALF // PARTS


def two_terms(x):
    hi = x.astype(BF16)
    lo = (x - hi.astype(F32)).astype(BF16)
    return hi, lo


def twice(x):
    hi, lo = two_terms(x)
    row = jnp.concatenate([hi, lo], axis=1)
    return jnp.concatenate([row, row], axis=0)


def dot(a, b):
    return jnp.dot(a, b, preferred_element_type=F32)


def folded(x):
    return x.reshape(-1, 8, x.shape[-1]).sum(axis=0)


def kernel(
    v_hbm, w_hbm, h_in, w_hbm_out, h_out,
    v_ref, w_in, w_new, in_sem, out_sem,
    h_ref, wcat, wtcat, hcat, cpart,
    xb, x_send, x_recv, token,
    nw, nsum, pair, psum, red, win, tot,
    p_send, p_recv, n_send, n_recv, s_send, s_recv, g_send, g_recv, q_send, q_recv,
):
    row = lax.axis_index("row")
    col = lax.axis_index("col")
    y, x = row // 4, row % 4
    z, core = col // 2, col % 2
    other = 1 - core
    kind, group = z % 8, z // 8

    def along_x(d):
        return (y * 4 + (x + d) % 4, col)

    def along_y(d):
        return (((y + d) % 4) * 4 + x, col)

    def along_z(d):
        return (row, ((z + d + 32) % 32) * 2 + core)

    partner = (row, z * 2 + other)
    strides = (16, 8, 24)
    near = [along_x(d) for d in (1, 2, 3)] + [along_y(d) for d in (1, 2, 3)]
    near += [partner, along_z(1), along_z(-1)]

    barrier = pltpu.get_barrier_semaphore()
    for p in near:
        pl.semaphore_signal(barrier, inc=1, device_id=p, device_id_type=MESH)

    w_load = pltpu.make_async_copy(w_hbm, w_in, in_sem.at[0])
    w_load.start()
    v_load = pltpu.make_async_copy(v_hbm, v_ref, in_sem.at[1])
    v_load.start()

    def tell(i):
        for d in (1 << i, -(1 << i)):
            pl.semaphore_signal(token.at[i], inc=1, device_id=along_z(d), device_id_type=MESH)

    def hear(i):
        pl.semaphore_wait(token.at[i], 2)

    def take_w(src):
        for b in range(8):
            rows = pl.ds(b * 128, 128)
            w = src[rows, :]
            hi, lo = two_terms(w)
            wcat[rows, 0:128] = hi
            wcat[rows, 128:256] = lo
            hi, lo = two_terms(w.T)
            wtcat[0:128, rows] = hi
            wtcat[128:256, rows] = lo
        cpart[...] = folded(src[...])

    def ratio_block(rows):
        both = dot(wcat[rows, :], hcat[...])
        ratio = v_ref[rows, :] / (both[:, 0:128] + both[:, 128:256])
        hi, lo = two_terms(ratio)
        return jnp.concatenate([hi, lo], axis=1)

    def local_numer():
        acc = jnp.zeros((256, 256), F32)
        for b in range(1024 // CHUNK):
            rows = pl.ds(b * CHUNK, CHUNK)
            acc += dot(wtcat[:, rows], ratio_block(rows))
        low = acc[128:256, 0:128] + acc[0:128, 128:256] + acc[128:256, 128:256]
        return acc[0:128, 0:128] + low

    mine = (x, y)
    ring = (along_x, along_y)

    def copies(slot, phase, half):
        axis = half if phase == 0 else 1 - half
        me = mine[axis]
        size = BLOCK if half == 0 else HALF
        out, into = [], []
        for d in (2, 1, 3):
            for at, got in ((me, out), ((me + d) % 4, into)):
                block = xb.at[slot, phase, half, at, pl.ds(0, size)]
                got.append(
                    pltpu.make_async_remote_copy(
                        src_ref=block,
                        dst_ref=block,
                        send_sem=x_send.at[slot, phase, half, d - 1],
                        recv_sem=x_recv.at[slot, phase, half, at],
                        device_id=ring[axis](d),
                        device_id_type=MESH,
                    )
                )
        return me, size, out, into

    def total_of(slot, phase, half, size):
        parts = [xb[slot, phase, half, i, 0:size] for i in range(4)]
        return (parts[0] + parts[1]) + (parts[2] + parts[3])

    def nothing():
        pass

    def update_h(slot, first=nothing, second=nothing, third=nothing):
        new = local_numer()
        plans = [[copies(slot, phase, half) for half in (0, 1)] for phase in (0, 1)]
        xb[slot, 0, 0, x, 0:HALF] = new[0:HALF]
        xb[slot, 0, 0, x, HALF:BLOCK] = cpart[...]
        xb[slot, 0, 1, y, 0:HALF] = new[HALF : 2 * HALF]
        first()
        for half in (0, 1):
            for c in plans[0][half][2]:
                c.start()
        for half in (0, 1):
            _, size, _, into = plans[0][half]
            for c in into:
                c.wait_recv()
            xb[slot, 1, half, plans[1][half][0], 0:size] = total_of(slot, 0, half, size)
            for c in plans[1][half][2]:
                c.start()
        second()
        for half in (0, 1):
            for c in plans[1][half][3]:
                c.wait_recv()
        third()
        top = total_of(slot, 1, 0, BLOCK)
        colsum = jnp.sum(top[HALF:BLOCK], axis=0, keepdims=True)
        over = jnp.broadcast_to(colsum, (128, 128)).T
        full = jnp.concatenate([top[0:HALF], total_of(slot, 1, 1, HALF)], axis=0)
        fresh = h_ref[...] * full / over
        h_ref[...] = fresh
        hcat[...] = twice(fresh)
        for phase in (0, 1):
            for half in (0, 1):
                for c in plans[phase][half][2]:
                    c.wait_send()

    def remote(src, dst, send, recv, to):
        return pltpu.make_async_remote_copy(
            src_ref=src, dst_ref=dst, send_sem=send, recv_sem=recv, device_id=to, device_id_type=MESH
        )

    def window(q):
        return (4 if q % 2 == 0 else -4, 3, -3, 2, -2, 1, -1)

    def span(q):
        return pl.ds(0, PART + EXTRA) if q == 0 else pl.ds(EXTRA, PART)

    def update_w():
        turned = h_ref[...].T
        weights = twice(turned)
        rowsum = folded(turned)
        nsum[...] = rowsum

        def numer_of(half):
            for b in range(512 // CHUNK):
                rows = pl.ds(pl.multiple_of(half * 512 + b * CHUNK, CHUNK), CHUNK)
                both = dot(ratio_block(rows), weights)
                both = both[:, 0:128] + both[:, 128:256]
                for i in range(CHUNK // PART):
                    place = b * (CHUNK // HALF) + i // PARTS
                    nw[half, i % PARTS, place] = both[i * PART : (i + 1) * PART]

        numer_of(other)
        give = [remote(nsum, psum, p_send.at[PARTS], p_recv.at[PARTS], partner)]
        for q in range(PARTS):
            give.append(remote(nw.at[other, q], pair.at[q], p_send.at[q], p_recv.at[q], partner))
        for c in give:
            c.start()
        numer_of(core)
        give[0].wait_recv()
        scatter, share, spread, over = [], [], [], []
        for q in range(PARTS):
            give[1 + q].wait_recv()
            for k in range(8):
                if q == 0:
                    red[q, k, 0:EXTRA] = rowsum + psum[...]
                red[q, k, EXTRA : EXTRA + PART] = nw[core, q, k] + pair[q, k]
            moves = []
            for i, d in enumerate(window(q)):
                moves.append(
                    remote(
                        red.at[q, (kind + d + 8) % 8, span(q)],
                        win.at[q, i, span(q)],
                        n_send.at[q, i],
                        n_recv.at[q, i],
                        along_z(d),
                    )
                )
            for c in moves:
                c.start()
            scatter.append(moves)
        for q in range(PARTS):
            for c in scatter[q]:
                c.wait_recv()
            acc = red[q, kind, span(q)]
            for i in range(7):
                acc += win[q, i, span(q)]
            tot[q, group, span(q)] = acc
            moves = []
            for i, d in enumerate(strides):
                block = tot.at[q, group, span(q)]
                moves.append(remote(block, block, s_send.at[q, i], s_recv.at[q, group], along_z(d)))
            for c in moves:
                c.start()
            share.append(moves)

        def part(q, which, owner):
            base = which * 512 + owner * HALF + q * PART
            return w_new.at[pl.ds(pl.multiple_of(base, PART), PART), :]

        below = None
        for q in range(PARTS):
            for i, d in enumerate(strides):
                at = (group + d // 8) % 4
                block = tot.at[q, at, span(q)]
                remote(block, block, s_send.at[q, i], s_recv.at[q, at], along_z(d)).wait_recv()
            full = [tot[q, i, span(q)] for i in range(4)]
            full = (full[0] + full[1]) + (full[2] + full[3])
            if q == 0:
                below = jnp.sum(full[0:EXTRA], axis=0, keepdims=True)
                full = full[EXTRA : EXTRA + PART]
            here = pl.ds(pl.multiple_of(core * 512 + kind * HALF + q * PART, PART), PART)
            w_new[here, :] = w_in[here, :] * full / below
            block = part(q, core, kind)
            moves = []
            for i, d in enumerate(window(q)):
                moves.append(remote(block, block, g_send.at[q, i], g_recv.at[q, i], along_z(d)))
            for c in moves:
                c.start()
            spread.append(moves)
            c = remote(block, block, q_send.at[q, 7], q_recv.at[q, 7], partner)
            c.start()
            over.append(c)
        for q in range(PARTS):
            for i in (5, 6, 3, 4, 1, 2, 0):
                spread[q][i].wait_recv()
                block = part(q, core, (kind - window(q)[i] + 8) % 8)
                c = remote(block, block, q_send.at[q, i], q_recv.at[q, i], partner)
                c.start()
                over.append(c)
        for c in over:
            c.wait_recv()
        for moves in scatter + share + spread + [give, over]:
            for c in moves:
                c.wait_send()

    def enter():
        pl.semaphore_wait(barrier, len(near))
        tell(0)

    def step(i):
        def then():
            hear(i)
            if i < 3:
                tell(i + 1)

        return then

    h_ref[...] = h_in[...]
    hcat[...] = twice(h_in[...])
    w_load.wait()
    take_w(w_in)
    v_load.wait()
    update_h(0, enter, step(0), step(1))
    update_h(1, nothing, step(2))
    update_h(0, nothing, nothing, step(3))
    update_w()
    w_store = pltpu.make_async_copy(w_new, w_hbm_out, out_sem)
    w_store.start()
    take_w(w_new)
    update_h(1)
    update_h(0)
    h_out[...] = h_ref[...]
    w_store.wait()


def pass_on(w_hbm, h_hbm, w_hbm_out, h_hbm_out, w, h, load, store):
    pieces = [(h_hbm, h, h_hbm_out)]
    for i in range(4):
        rows = pl.ds(i * 256, 256)
        pieces.append((w_hbm.at[rows], w.at[rows], w_hbm_out.at[rows]))
    ins = [pltpu.make_async_copy(a, b, load.at[i]) for i, (a, b, _) in enumerate(pieces)]
    outs = [pltpu.make_async_copy(b, c, store.at[i]) for i, (_, b, c) in enumerate(pieces)]
    for c in ins:
        c.start()
    for a, b in zip(ins, outs):
        a.wait()
        b.start()
    for c in outs:
        c.wait()


def per_device(spectra, factor_w, factor_h):
    vmem = pl.BlockSpec(memory_space=pltpu.VMEM)
    hbm = pl.BlockSpec(memory_space=pl.ANY)
    dma = pltpu.SemaphoreType.DMA
    shapes = (jax.ShapeDtypeStruct((1024, 128), F32), jax.ShapeDtypeStruct((128, 128), F32))
    room = PART + EXTRA
    w, h = pl.pallas_call(
        kernel,
        out_shape=shapes,
        in_specs=[hbm, hbm, vmem],
        out_specs=(hbm, vmem),
        scratch_shapes=[
            pltpu.VMEM((1024, 128), F32),
            pltpu.VMEM((1024, 128), F32),
            pltpu.VMEM((1024, 128), F32),
            dma((2,)),
            dma,
            pltpu.VMEM((128, 128), F32),
            pltpu.VMEM((1024, 256), BF16),
            pltpu.VMEM((256, 1024), BF16),
            pltpu.VMEM((256, 256), BF16),
            pltpu.VMEM((EXTRA, 128), F32),
            pltpu.VMEM((2, 2, 2, 4, BLOCK, 128), F32),
            dma((2, 2, 2, 3)),
            dma((2, 2, 2, 4)),
            pltpu.SemaphoreType.REGULAR((4,)),
            pltpu.VMEM((2, PARTS, 8, PART, 128), F32),
            pltpu.VMEM((EXTRA, 128), F32),
            pltpu.VMEM((PARTS, 8, PART, 128), F32),
            pltpu.VMEM((EXTRA, 128), F32),
            pltpu.VMEM((PARTS, 8, room, 128), F32),
            pltpu.VMEM((PARTS, 7, room, 128), F32),
            pltpu.VMEM((PARTS, 4, room, 128), F32),
            dma((PARTS + 1,)), dma((PARTS + 1,)),
            dma((PARTS, 7)), dma((PARTS, 7)),
            dma((PARTS, 3)), dma((PARTS, 4)),
            dma((PARTS, 7)), dma((PARTS, 7)),
            dma((PARTS, 8)), dma((PARTS, 8)),
        ],
        compiler_params=pltpu.CompilerParams(collective_id=0, has_side_effects=True),
        name="nmf",
    )(spectra, factor_w, factor_h)
    return pl.pallas_call(
        pass_on,
        out_shape=shapes,
        in_specs=[hbm, hbm],
        out_specs=(hbm, hbm),
        scratch_shapes=[
            pltpu.VMEM((1024, 128), F32),
            pltpu.VMEM((128, 128), F32),
            dma((5,)),
            dma((5,)),
        ],
        name="pass_on",
    )(w, h)


def solution(mesh):
    return jax.shard_map(
        per_device,
        mesh=mesh,
        in_specs=(P("row", "col"), P("row", None), P(None, "col")),
        out_specs=(P("row", None), P(None, "col")),
        check_vma=False,
    )
```

```python
import functools

import jax
import jax.numpy as jnp
from jax import lax
from jax.experimental import pallas as pl
from jax.experimental.pallas import tpu as pltpu
from jax.sharding import PartitionSpec as P

MESH = pl.DeviceIdType.MESH
F32 = jnp.float32
BF16 = jnp.bfloat16
HALF = 64
EXTRA = 8
SUB = 2
PIECES = 2 * SUB
PIECE = 128 // PIECES
CHUNK = 256
PARTS = 2
PART = HALF // PARTS


def two_terms(x):
    hi = x.astype(BF16)
    lo = (x - hi.astype(F32)).astype(BF16)
    return hi, lo


def twice(x):
    hi, lo = two_terms(x)
    row = jnp.concatenate([hi, lo], axis=1)
    return jnp.concatenate([row, row], axis=0)


def dot(a, b):
    return jnp.dot(a, b, preferred_element_type=F32)


def folded(x):
    return x.reshape(-1, 8, x.shape[-1]).sum(axis=0)


def kernel(
    v_hbm, w_hbm, h_hbm, w_out, h_out,
    v_ref, w_in, w_new, in_sem, out_sem,
    h_ref, wcat, wtcat, hcat, cpart,
    xb, x_send, x_recv, token,
    nw, nsum, pair, psum, red, win, tot,
    p_send, p_recv, n_send, n_recv, s_send, s_recv, g_send, g_recv, q_send, q_recv,
):
    row = lax.axis_index("row")
    col = lax.axis_index("col")
    y, x = row // 4, row % 4
    z, core = col // 2, col % 2
    other = 1 - core
    kind, group = z % 8, z // 8

    def along_x(d):
        return (y * 4 + (x + d) % 4, col)

    def along_y(d):
        return (((y + d) % 4) * 4 + x, col)

    def along_z(d):
        return (row, ((z + d + 32) % 32) * 2 + core)

    partner = (row, z * 2 + other)
    near = [along_x(d) for d in (1, 2, 3)] + [along_y(d) for d in (1, 2, 3)]
    near += [partner, along_z(1), along_z(-1)]

    barrier = pltpu.get_barrier_semaphore()
    for p in near:
        pl.semaphore_signal(barrier, inc=1, device_id=p, device_id_type=MESH)

    w_load = pltpu.make_async_copy(w_hbm, w_in, in_sem.at[0])
    w_load.start()
    h_load = pltpu.make_async_copy(h_hbm, h_ref, in_sem.at[2])
    h_load.start()
    v_load = pltpu.make_async_copy(v_hbm, v_ref, in_sem.at[1])
    v_load.start()

    def tell(i):
        for d in (1 << i, -(1 << i)):
            pl.semaphore_signal(token.at[i], inc=1, device_id=along_z(d), device_id_type=MESH)

    def hear(i):
        pl.semaphore_wait(token.at[i], 2)

    def take_w(src):
        for b in range(8):
            rows = pl.ds(b * 128, 128)
            w = src[rows, :]
            hi, lo = two_terms(w)
            wcat[rows, 0:128] = hi
            wcat[rows, 128:256] = lo
            hi, lo = two_terms(w.T)
            wtcat[0:128, rows] = hi
            wtcat[128:256, rows] = lo
        cpart[...] = folded(src[...])

    def ratio_block(rows):
        both = dot(wcat[rows, :], hcat[...])
        ratio = v_ref[rows, :] / (both[:, 0:128] + both[:, 128:256])
        hi, lo = two_terms(ratio)
        return jnp.concatenate([hi, lo], axis=1)

    def local_numer():
        acc = jnp.zeros((256, 256), F32)
        for b in range(1024 // CHUNK):
            rows = pl.ds(b * CHUNK, CHUNK)
            acc += dot(wtcat[:, rows], ratio_block(rows))
        low = acc[128:256, 0:128] + acc[0:128, 128:256] + acc[128:256, 128:256]
        return acc[0:128, 0:128] + low

    mine = (x, y)
    ring = (along_x, along_y)

    def rows_of(p):
        return PIECE + EXTRA if p == 0 else PIECE

    def copies(slot, phase, p):
        axis = (p + phase) % 2
        me = mine[axis]
        out, into = [], []
        for d in (2, 1, 3):
            for at, got in ((me, out), ((me + d) % 4, into)):
                block = xb.at[slot, phase, p, at, pl.ds(0, rows_of(p))]
                got.append(
                    pltpu.make_async_remote_copy(
                        src_ref=block,
                        dst_ref=block,
                        send_sem=x_send.at[slot, phase, p, d - 1],
                        recv_sem=x_recv.at[slot, phase, p, at],
                        device_id=ring[axis](d),
                        device_id_type=MESH,
                    )
                )
        return me, out, into

    def total_of(slot, phase, p):
        parts = [xb[slot, phase, p, i, 0 : rows_of(p)] for i in range(4)]
        return (parts[0] + parts[1]) + (parts[2] + parts[3])

    def nothing():
        pass

    def update_h(slot, first=nothing, second=nothing, third=nothing):
        new = local_numer()
        plans = [[copies(slot, phase, p) for p in range(PIECES)] for phase in (0, 1)]
        for p in range(PIECES):
            xb[slot, 0, p, mine[p % 2], 0:PIECE] = new[p * PIECE : (p + 1) * PIECE]
        xb[slot, 0, 0, x, PIECE : PIECE + EXTRA] = cpart[...]
        first()
        for _, out, _ in plans[0]:
            for c in out:
                c.start()
        for p in range(PIECES):
            for c in plans[0][p][2]:
                c.wait_recv()
            me, out, _ = plans[1][p]
            xb[slot, 1, p, me, 0 : rows_of(p)] = total_of(slot, 0, p)
            for c in out:
                c.start()
        second()
        full = []
        for p in range(PIECES):
            for c in plans[1][p][2]:
                c.wait_recv()
            full.append(total_of(slot, 1, p))
        third()
        colsum = jnp.sum(full[0][PIECE:], axis=0, keepdims=True)
        over = jnp.broadcast_to(colsum, (128, 128)).T
        full[0] = full[0][0:PIECE]
        fresh = h_ref[...] * jnp.concatenate(full, axis=0) / over
        h_ref[...] = fresh
        hcat[...] = twice(fresh)
        for plan_of in plans:
            for _, out, _ in plan_of:
                for c in out:
                    c.wait_send()

    def remote(src, dst, send, recv, to):
        return pltpu.make_async_remote_copy(
            src_ref=src, dst_ref=dst, send_sem=send, recv_sem=recv, device_id=to, device_id_type=MESH
        )

    def window(q):
        return (4 if q % 2 == 0 else -4, 3, -3, 2, -2, 1, -1)

    def span(q):
        return pl.ds(0, PART + EXTRA) if q == 0 else pl.ds(EXTRA, PART)

    def update_w():
        turned = h_ref[...].T
        weights = twice(turned)
        rowsum = folded(turned)
        nsum[...] = rowsum

        def numer_of(half):
            for b in range(512 // CHUNK):
                rows = pl.ds(pl.multiple_of(half * 512 + b * CHUNK, CHUNK), CHUNK)
                both = dot(ratio_block(rows), weights)
                both = both[:, 0:128] + both[:, 128:256]
                for i in range(CHUNK // PART):
                    place = b * (CHUNK // HALF) + i // PARTS
                    nw[half, i % PARTS, place] = both[i * PART : (i + 1) * PART]

        def swap(q, step):
            way = group + q + step
            to = along_z(8 - 16 * (way % 2))
            return remote(
                tot.at[q, 2 * step, span(q)],
                tot.at[q, 2 * step + 1, span(q)],
                s_send.at[q, step],
                s_recv.at[q, step],
                to,
            )

        numer_of(other)
        give = [remote(nsum, psum, p_send.at[PARTS], p_recv.at[PARTS], partner)]
        for q in range(PARTS):
            give.append(remote(nw.at[other, q], pair.at[q], p_send.at[q], p_recv.at[q], partner))
        for c in give:
            c.start()
        numer_of(core)
        give[0].wait_recv()
        scatter, share, spread, over = [], [], [], []
        for q in range(PARTS):
            give[1 + q].wait_recv()
            for k in range(8):
                if q == 0:
                    red[q, k, 0:EXTRA] = rowsum + psum[...]
                red[q, k, EXTRA : EXTRA + PART] = nw[core, q, k] + pair[q, k]
            moves = []
            for i, d in enumerate(window(q)):
                moves.append(
                    remote(
                        red.at[q, (kind + d + 8) % 8, span(q)],
                        win.at[q, i, span(q)],
                        n_send.at[q, i],
                        n_recv.at[q, i],
                        along_z(d),
                    )
                )
            for c in moves:
                c.start()
            scatter.append(moves)
        for q in range(PARTS):
            for c in scatter[q]:
                c.wait_recv()
            acc = red[q, kind, span(q)]
            for i in range(7):
                acc += win[q, i, span(q)]
            tot[q, 0, span(q)] = acc
            share.append([swap(q, 0)])
            share[q][0].start()
        for q in range(PARTS):
            share[q][0].wait_recv()
            tot[q, 2, span(q)] = tot[q, 0, span(q)] + tot[q, 1, span(q)]
            share[q].append(swap(q, 1))
            share[q][1].start()

        def part(q, which, owner):
            base = which * 512 + owner * HALF + q * PART
            return w_new.at[pl.ds(pl.multiple_of(base, PART), PART), :]

        below = None
        for q in range(PARTS):
            share[q][1].wait_recv()
            full = tot[q, 2, span(q)] + tot[q, 3, span(q)]
            if q == 0:
                below = jnp.sum(full[0:EXTRA], axis=0, keepdims=True)
                full = full[EXTRA : EXTRA + PART]
            here = pl.ds(pl.multiple_of(core * 512 + kind * HALF + q * PART, PART), PART)
            w_new[here, :] = w_in[here, :] * full / below
            block = part(q, core, kind)
            moves = []
            for i, d in enumerate(window(q)):
                moves.append(remote(block, block, g_send.at[q, i], g_recv.at[q, i], along_z(d)))
            for c in moves:
                c.start()
            spread.append(moves)
            c = remote(block, block, q_send.at[q, 7], q_recv.at[q, 7], partner)
            c.start()
            over.append(c)
        for q in range(PARTS):
            for i in (5, 6, 3, 4, 1, 2, 0):
                spread[q][i].wait_recv()
                block = part(q, core, (kind - window(q)[i] + 8) % 8)
                c = remote(block, block, q_send.at[q, i], q_recv.at[q, i], partner)
                c.start()
                over.append(c)
        for c in over:
            c.wait_recv()
        for moves in scatter + share + spread + [give, over]:
            for c in moves:
                c.wait_send()

    def enter():
        pl.semaphore_wait(barrier, len(near))
        tell(0)

    def step(i):
        def then():
            hear(i)
            if i < 2:
                tell(i + 1)

        return then

    w_load.wait()
    take_w(w_in)
    h_load.wait()
    hcat[...] = twice(h_ref[...])
    v_load.wait()
    update_h(0, enter, step(0), step(1))
    update_h(1, nothing, step(2))
    update_h(0)
    update_w()
    w_store = pltpu.make_async_copy(w_new, w_out, out_sem)
    w_store.start()
    take_w(w_new)
    update_h(1)
    update_h(0)
    h_out[...] = h_ref[...]
    w_store.wait()


def pass_on(w, h, w_hbm_out, h_hbm_out, store):
    outs = [pltpu.make_async_copy(h, h_hbm_out, store.at[4])]
    for i in range(4):
        rows = pl.ds(i * 256, 256)
        outs.append(pltpu.make_async_copy(w.at[rows], w_hbm_out.at[rows], store.at[i]))
    for c in outs:
        c.start()
    for c in outs:
        c.wait()


def per_device(spectra, factor_w, factor_h):
    vmem = pl.BlockSpec(memory_space=pltpu.VMEM)
    hbm = pl.BlockSpec(memory_space=pl.ANY)
    dma = pltpu.SemaphoreType.DMA
    shapes = (jax.ShapeDtypeStruct((1024, 128), F32), jax.ShapeDtypeStruct((128, 128), F32))
    room = PART + EXTRA
    w, h = pl.pallas_call(
        kernel,
        out_shape=shapes,
        in_specs=[pl.BlockSpec(memory_space=pltpu.HBM)] * 3,
        out_specs=(vmem, vmem),
        scratch_shapes=[
            pltpu.VMEM((1024, 128), F32),
            pltpu.VMEM((1024, 128), F32),
            pltpu.VMEM((1024, 128), F32),
            dma((3,)),
            dma,
            pltpu.VMEM((128, 128), F32),
            pltpu.VMEM((1024, 256), BF16),
            pltpu.VMEM((256, 1024), BF16),
            pltpu.VMEM((256, 256), BF16),
            pltpu.VMEM((EXTRA, 128), F32),
            pltpu.VMEM((2, 2, PIECES, 4, PIECE + EXTRA, 128), F32),
            dma((2, 2, PIECES, 3)),
            dma((2, 2, PIECES, 4)),
            pltpu.SemaphoreType.REGULAR((3,)),
            pltpu.VMEM((2, PARTS, 8, PART, 128), F32),
            pltpu.VMEM((EXTRA, 128), F32),
            pltpu.VMEM((PARTS, 8, PART, 128), F32),
            pltpu.VMEM((EXTRA, 128), F32),
            pltpu.VMEM((PARTS, 8, room, 128), F32),
            pltpu.VMEM((PARTS, 7, room, 128), F32),
            pltpu.VMEM((PARTS, 4, room, 128), F32),
            dma((PARTS + 1,)), dma((PARTS + 1,)),
            dma((PARTS, 7)), dma((PARTS, 7)),
            dma((PARTS, 2)), dma((PARTS, 2)),
            dma((PARTS, 7)), dma((PARTS, 7)),
            dma((PARTS, 8)), dma((PARTS, 8)),
        ],
        compiler_params=pltpu.CompilerParams(
            collective_id=0, has_side_effects=True, vmem_limit_bytes=16 * 2**20
        ),
        name="nmf",
    )(*(pltpu.with_memory_space_constraint(a, pltpu.HBM) for a in (spectra, factor_w, factor_h)))
    return pl.pallas_call(
        pass_on,
        out_shape=shapes,
        in_specs=[vmem, vmem],
        out_specs=(hbm, hbm),
        scratch_shapes=[dma((5,))],
        compiler_params=pltpu.CompilerParams(vmem_limit_bytes=8 * 2**20),
        name="pass_on",
    )(w, h)


def solution(mesh):
    return jax.shard_map(
        per_device,
        mesh=mesh,
        in_specs=(P("row", "col"), P("row", None), P(None, "col")),
        out_specs=(P("row", None), P(None, "col")),
        check_vma=False,
    )
```

```python
import functools

import jax
import jax.numpy as jnp
from jax import lax
from jax.experimental import pallas as pl
from jax.experimental.pallas import tpu as pltpu
from jax.sharding import PartitionSpec as P

MESH = pl.DeviceIdType.MESH
F32 = jnp.float32
BF16 = jnp.bfloat16
HALF = 64
EXTRA = 8
SUB = 2
PIECES = 2 * SUB
PIECE = 128 // PIECES
CHUNK = 256
PARTS = 4
PART = HALF // PARTS


def two_terms(x):
    hi = x.astype(BF16)
    lo = (x - hi.astype(F32)).astype(BF16)
    return hi, lo


def twice(x):
    hi, lo = two_terms(x)
    row = jnp.concatenate([hi, lo], axis=1)
    return jnp.concatenate([row, row], axis=0)


def dot(a, b):
    return jnp.dot(a, b, preferred_element_type=F32)


def folded(x):
    return x.reshape(-1, 8, x.shape[-1]).sum(axis=0)


def kernel(
    v_hbm, w_hbm, h_hbm, w_out, h_out,
    v_ref, w_in, w_new, in_sem, out_sem,
    h_ref, wcat, wtcat, hcat, cpart, inverse,
    xb, x_send, x_recv, token,
    nw, nsum, pair, psum, red, win, tot,
    p_send, p_recv, n_send, n_recv, s_send, s_recv, g_send, g_recv, q_send, q_recv,
):
    row = lax.axis_index("row")
    col = lax.axis_index("col")
    y, x = row // 4, row % 4
    z, core = col // 2, col % 2
    other = 1 - core
    kind, group = z % 8, z // 8

    def along_x(d):
        return (y * 4 + (x + d) % 4, col)

    def along_y(d):
        return (((y + d) % 4) * 4 + x, col)

    def along_z(d):
        return (row, ((z + d + 32) % 32) * 2 + core)

    partner = (row, z * 2 + other)
    near = [along_x(d) for d in (1, 2, 3)] + [along_y(d) for d in (1, 2, 3)]
    near += [partner, along_z(1), along_z(-1)]

    barrier = pltpu.get_barrier_semaphore()
    for p in near:
        pl.semaphore_signal(barrier, inc=1, device_id=p, device_id_type=MESH)

    w_load = pltpu.make_async_copy(w_hbm, w_in, in_sem.at[0])
    w_load.start()
    h_load = pltpu.make_async_copy(h_hbm, h_ref, in_sem.at[2])
    h_load.start()
    v_load = pltpu.make_async_copy(v_hbm, v_ref, in_sem.at[1])
    v_load.start()

    def tell(i):
        for d in (1 << i, -(1 << i)):
            pl.semaphore_signal(token.at[i], inc=1, device_id=along_z(d), device_id_type=MESH)

    def hear(i):
        pl.semaphore_wait(token.at[i], 2)

    pending = []

    def settle():
        for c in pending:
            c.wait_send()
        pending.clear()

    def take_w(src, blocks):
        for b in blocks:
            rows = pl.ds(b, 128)
            w = src[rows, :]
            hi, lo = two_terms(w)
            wcat[rows, 0:128] = hi
            wcat[rows, 128:256] = lo
            hi, lo = two_terms(w.T)
            wtcat[0:128, rows] = hi
            wtcat[128:256, rows] = lo

    def ratio_block(rows):
        both = dot(wcat[rows, :], hcat[...])
        ratio = v_ref[rows, :] / (both[:, 0:128] + both[:, 128:256])
        hi, lo = two_terms(ratio)
        return jnp.concatenate([hi, lo], axis=1)

    def starts_of(half, size):
        return [pl.multiple_of(half * 512 + i, size) for i in range(0, 512, size)]

    def products(bases):
        acc = None
        for base in bases:
            rows = pl.ds(base, CHUNK)
            one = dot(wtcat[:, rows], ratio_block(rows))
            acc = one if acc is None else acc + one
        return acc

    def local_numer():
        return products(range(0, 1024, CHUNK))

    def joined(acc):
        low = acc[128:256, 0:128] + acc[0:128, 128:256] + acc[128:256, 128:256]
        return acc[0:128, 0:128] + low

    mine = (x, y)
    ring = (along_x, along_y)

    def rows_of(p, new_w):
        return PIECE + EXTRA if p == 0 and new_w else PIECE

    def copies(slot, phase, p, new_w):
        axis = (p + phase) % 2
        me = mine[axis]
        out, into = [], []
        for d in (2, 1, 3):
            for at, got in ((me, out), ((me + d) % 4, into)):
                block = xb.at[slot, phase, p, at, pl.ds(0, rows_of(p, new_w))]
                got.append(
                    pltpu.make_async_remote_copy(
                        src_ref=block,
                        dst_ref=block,
                        send_sem=x_send.at[slot, phase, p, d - 1],
                        recv_sem=x_recv.at[slot, phase, p, at],
                        device_id=ring[axis](d),
                        device_id_type=MESH,
                    )
                )
        return me, out, into

    def total_of(slot, phase, p, new_w):
        parts = [xb[slot, phase, p, i, 0 : rows_of(p, new_w)] for i in range(4)]
        return (parts[0] + parts[1]) + (parts[2] + parts[3])

    def nothing():
        pass

    def update_h(slot, numer=local_numer, new_w=False, first=nothing, second=nothing, third=nothing):
        new = joined(numer())
        plans = [[copies(slot, phase, p, new_w) for p in range(PIECES)] for phase in (0, 1)]
        for p in range(PIECES):
            xb[slot, 0, p, mine[p % 2], 0:PIECE] = new[p * PIECE : (p + 1) * PIECE]
        if new_w:
            xb[slot, 0, 0, x, PIECE : PIECE + EXTRA] = cpart[...]
        first()
        for _, out, _ in plans[0]:
            for c in out:
                c.start()
        settle()
        for p in range(PIECES):
            for c in plans[0][p][2]:
                c.wait_recv()
            me, out, _ = plans[1][p]
            xb[slot, 1, p, me, 0 : rows_of(p, new_w)] = total_of(slot, 0, p, new_w)
            for c in out:
                c.start()
        second()
        for _, out, _ in plans[0]:
            for c in out:
                c.wait_send()
        for p in range(PIECES):
            for c in plans[1][p][2]:
                c.wait_recv()
            full = total_of(slot, 1, p, new_w)
            if p == 0 and new_w:
                colsum = jnp.sum(full[PIECE:], axis=0, keepdims=True)
                inverse[...] = 1.0 / jnp.broadcast_to(colsum, (128, 128)).T
                full = full[0:PIECE]
            rows = slice(p * PIECE, (p + 1) * PIECE)
            fresh = h_ref[rows] * full * inverse[rows]
            h_ref[rows] = fresh
            hi, lo = two_terms(fresh)
            for base in (0, 128):
                again = slice(base + p * PIECE, base + (p + 1) * PIECE)
                hcat[again, 0:128] = hi
                hcat[again, 128:256] = lo
        third()
        for _, out, _ in plans[1]:
            pending.extend(out)

    def remote(src, dst, send, recv, to):
        return pltpu.make_async_remote_copy(
            src_ref=src, dst_ref=dst, send_sem=send, recv_sem=recv, device_id=to, device_id_type=MESH
        )

    def window(q):
        return (4 if q % 2 == 0 else -4, 3, -3, 2, -2, 1, -1)

    def span(q):
        return pl.ds(0, PART + EXTRA) if q == 0 else pl.ds(EXTRA, PART)

    def update_w():
        turned = h_ref[...].T
        weights = twice(turned)
        rowsum = folded(turned)
        nsum[...] = rowsum

        def numer_of(half, b):
            rows = pl.ds(pl.multiple_of(half * 512 + b * CHUNK, CHUNK), CHUNK)
            both = dot(ratio_block(rows), weights)
            both = both[:, 0:128] + both[:, 128:256]
            for i in range(CHUNK // PART):
                place = b * (CHUNK // HALF) + i // PARTS
                nw[half, i % PARTS, place] = both[i * PART : (i + 1) * PART]

        def swap(q, step):
            way = group + q + step
            to = along_z(8 - 16 * (way % 2))
            return remote(
                tot.at[q, 2 * step, span(q)],
                tot.at[q, 2 * step + 1, span(q)],
                s_send.at[q, step],
                s_recv.at[q, step],
                to,
            )

        blocks = 512 // CHUNK
        each = 8 // blocks
        sums = remote(nsum, psum, p_send.at[PARTS * blocks], p_recv.at[PARTS * blocks], partner)
        sums.start()
        give = []
        for b in range(blocks):
            numer_of(other, b)
            for q in range(PARTS):
                at = pl.ds(b * each, each)
                i = b * PARTS + q
                c = remote(nw.at[other, q, at], pair.at[q, at], p_send.at[i], p_recv.at[i], partner)
                c.start()
                give.append(c)
        settle()
        for b in range(blocks):
            numer_of(core, b)
        sums.wait_recv()
        scatter, share, spread, over = [], [], [], []
        for q in range(PARTS):
            for b in range(blocks):
                give[b * PARTS + q].wait_recv()
            for k in range(8):
                if q == 0:
                    red[q, k, 0:EXTRA] = rowsum + psum[...]
                red[q, k, EXTRA : EXTRA + PART] = nw[core, q, k] + pair[q, k]
            moves = []
            for i, d in enumerate(window(q)):
                moves.append(
                    remote(
                        red.at[q, (kind + d + 8) % 8, span(q)],
                        win.at[q, i, span(q)],
                        n_send.at[q, i],
                        n_recv.at[q, i],
                        along_z(d),
                    )
                )
            for c in moves:
                c.start()
            scatter.append(moves)
        for q in range(PARTS):
            for c in scatter[q]:
                c.wait_recv()
            acc = red[q, kind, span(q)]
            for i in range(7):
                acc += win[q, i, span(q)]
            tot[q, 0, span(q)] = acc
            share.append([swap(q, 0)])
            share[q][0].start()
        for q in range(PARTS):
            share[q][0].wait_recv()
            tot[q, 2, span(q)] = tot[q, 0, span(q)] + tot[q, 1, span(q)]
            share[q].append(swap(q, 1))
            share[q][1].start()

        def part(q, which, owner):
            base = which * 512 + owner * HALF + q * PART
            return w_new.at[pl.ds(pl.multiple_of(base, PART), PART), :]

        below = None
        for q in range(PARTS):
            share[q][1].wait_recv()
            full = tot[q, 2, span(q)] + tot[q, 3, span(q)]
            if q == 0:
                below = jnp.sum(full[0:EXTRA], axis=0, keepdims=True)
                full = full[EXTRA : EXTRA + PART]
            here = pl.ds(pl.multiple_of(core * 512 + kind * HALF + q * PART, PART), PART)
            w_new[here, :] = w_in[here, :] * full / below
            block = part(q, core, kind)
            moves = []
            for i, d in enumerate(window(q)):
                moves.append(remote(block, block, g_send.at[q, i], g_recv.at[q, i], along_z(d)))
            for c in moves:
                c.start()
            spread.append(moves)
            c = remote(block, block, q_send.at[q, 7], q_recv.at[q, 7], partner)
            c.start()
            over.append(c)
        for q in range(PARTS):
            for i in (5, 6, 3, 4, 1, 2, 0):
                spread[q][i].wait_recv()
                block = part(q, core, (kind - window(q)[i] + 8) % 8)
                c = remote(block, block, q_send.at[q, i], q_recv.at[q, i], partner)
                c.start()
                over.append(c)
        pending.append(sums)
        for moves in scatter + share + spread + [give, over]:
            pending.extend(moves)

        def numer():
            take_w(w_new, starts_of(core, 128))
            acc = products(starts_of(core, CHUNK))
            for c in over:
                c.wait_recv()
            w_store.start()
            take_w(w_new, starts_of(other, 128))
            cpart[...] = folded(w_new[...])
            return acc + products(starts_of(other, CHUNK))

        return numer

    def enter():
        pl.semaphore_wait(barrier, len(near))
        tell(0)

    def step(i):
        def then():
            hear(i)
            if i < 2:
                tell(i + 1)

        return then

    w_store = pltpu.make_async_copy(w_new, w_out, out_sem)
    w_load.wait()
    take_w(w_in, range(0, 1024, 128))
    cpart[...] = folded(w_in[...])
    h_load.wait()
    hcat[...] = twice(h_ref[...])
    v_load.wait()
    update_h(0, local_numer, True, enter, step(0), step(1))
    update_h(1, second=step(2))
    update_h(0)
    numer = update_w()
    update_h(1, numer, True)
    update_h(0)
    h_out[...] = h_ref[...]
    settle()
    w_store.wait()


def pass_on(w, h, w_hbm_out, h_hbm_out, store):
    outs = [pltpu.make_async_copy(h, h_hbm_out, store.at[4])]
    for i in range(4):
        rows = pl.ds(i * 256, 256)
        outs.append(pltpu.make_async_copy(w.at[rows], w_hbm_out.at[rows], store.at[i]))
    for c in outs:
        c.start()
    for c in outs:
        c.wait()


def per_device(spectra, factor_w, factor_h):
    vmem = pl.BlockSpec(memory_space=pltpu.VMEM)
    hbm = pl.BlockSpec(memory_space=pl.ANY)
    dma = pltpu.SemaphoreType.DMA
    shapes = (jax.ShapeDtypeStruct((1024, 128), F32), jax.ShapeDtypeStruct((128, 128), F32))
    room = PART + EXTRA
    w, h = pl.pallas_call(
        kernel,
        out_shape=shapes,
        in_specs=[pl.BlockSpec(memory_space=pltpu.HBM)] * 3,
        out_specs=(vmem, vmem),
        scratch_shapes=[
            pltpu.VMEM((1024, 128), F32),
            pltpu.VMEM((1024, 128), F32),
            pltpu.VMEM((1024, 128), F32),
            dma((3,)),
            dma,
            pltpu.VMEM((128, 128), F32),
            pltpu.VMEM((1024, 256), BF16),
            pltpu.VMEM((256, 1024), BF16),
            pltpu.VMEM((256, 256), BF16),
            pltpu.VMEM((EXTRA, 128), F32),
            pltpu.VMEM((128, 128), F32),
            pltpu.VMEM((2, 2, PIECES, 4, PIECE + EXTRA, 128), F32),
            dma((2, 2, PIECES, 3)),
            dma((2, 2, PIECES, 4)),
            pltpu.SemaphoreType.REGULAR((3,)),
            pltpu.VMEM((2, PARTS, 8, PART, 128), F32),
            pltpu.VMEM((EXTRA, 128), F32),
            pltpu.VMEM((PARTS, 8, PART, 128), F32),
            pltpu.VMEM((EXTRA, 128), F32),
            pltpu.VMEM((PARTS, 8, room, 128), F32),
            pltpu.VMEM((PARTS, 7, room, 128), F32),
            pltpu.VMEM((PARTS, 4, room, 128), F32),
            dma((PARTS * 512 // CHUNK + 1,)), dma((PARTS * 512 // CHUNK + 1,)),
            dma((PARTS, 7)), dma((PARTS, 7)),
            dma((PARTS, 2)), dma((PARTS, 2)),
            dma((PARTS, 7)), dma((PARTS, 7)),
            dma((PARTS, 8)), dma((PARTS, 8)),
        ],
        compiler_params=pltpu.CompilerParams(
            collective_id=0, has_side_effects=True, vmem_limit_bytes=16 * 2**20
        ),
        name="nmf",
    )(*(pltpu.with_memory_space_constraint(a, pltpu.HBM) for a in (spectra, factor_w, factor_h)))
    return pl.pallas_call(
        pass_on,
        out_shape=shapes,
        in_specs=[vmem, vmem],
        out_specs=(hbm, hbm),
        scratch_shapes=[dma((5,))],
        compiler_params=pltpu.CompilerParams(vmem_limit_bytes=8 * 2**20),
        name="pass_on",
    )(w, h)


def solution(mesh):
    return jax.shard_map(
        per_device,
        mesh=mesh,
        in_specs=(P("row", "col"), P("row", None), P(None, "col")),
        out_specs=(P("row", None), P(None, "col")),
        check_vma=False,
    )
```

```python
import functools

import jax
import jax.numpy as jnp
from jax import lax
from jax.experimental import pallas as pl
from jax.experimental.pallas import tpu as pltpu
from jax.sharding import PartitionSpec as P

MESH = pl.DeviceIdType.MESH
F32 = jnp.float32
BF16 = jnp.bfloat16
HALF = 64
EXTRA = 8
SUB = 2
PIECES = 2 * SUB
PIECE = 128 // PIECES
CHUNK = 256
PARTS = 4
PART = HALF // PARTS


def two_terms(x):
    hi = x.astype(BF16)
    lo = (x - hi.astype(F32)).astype(BF16)
    return hi, lo


def twice(x):
    hi, lo = two_terms(x)
    row = jnp.concatenate([hi, lo], axis=1)
    return jnp.concatenate([row, row], axis=0)


def dot(a, b):
    return jnp.dot(a, b, preferred_element_type=F32)


def folded(x):
    return x.reshape(-1, 8, x.shape[-1]).sum(axis=0)


def kernel(
    v_hbm, w_hbm, h_hbm, w_out, h_out,
    v_ref, w_in, w_new, in_sem, out_sem,
    h_ref, wcat, wtcat, hcat, cpart, inverse,
    xb, x_send, x_recv, token,
    nw, nsum, pair, psum, red, win, tot,
    p_send, p_recv, n_send, n_recv, s_send, s_recv, g_send, g_recv, q_send, q_recv,
):
    row = lax.axis_index("row")
    col = lax.axis_index("col")
    y, x = row // 4, row % 4
    z, core = col // 2, col % 2
    other = 1 - core
    kind, group = z % 8, z // 8

    def along_x(d):
        return (y * 4 + (x + d) % 4, col)

    def along_y(d):
        return (((y + d) % 4) * 4 + x, col)

    def along_z(d):
        return (row, ((z + d + 32) % 32) * 2 + core)

    partner = (row, z * 2 + other)
    near = [along_x(d) for d in (1, 2, 3)] + [along_y(d) for d in (1, 2, 3)]
    near += [partner, along_z(1), along_z(-1)]

    barrier = pltpu.get_barrier_semaphore()
    for p in near:
        pl.semaphore_signal(barrier, inc=1, device_id=p, device_id_type=MESH)

    w_load = pltpu.make_async_copy(w_hbm, w_in, in_sem.at[0])
    w_load.start()
    h_load = pltpu.make_async_copy(h_hbm, h_ref, in_sem.at[2])
    h_load.start()
    v_load = pltpu.make_async_copy(v_hbm, v_ref, in_sem.at[1])
    v_load.start()

    def tell(i):
        for d in (1 << i, -(1 << i)):
            pl.semaphore_signal(token.at[i], inc=1, device_id=along_z(d), device_id_type=MESH)

    def hear(i):
        pl.semaphore_wait(token.at[i], 2)

    pending = []

    def settle():
        for c in pending:
            c.wait_send()
        pending.clear()

    def take_w(src, blocks):
        for b in blocks:
            rows = pl.ds(b, 128)
            w = src[rows, :]
            hi, lo = two_terms(w)
            wcat[rows, 0:128] = hi
            wcat[rows, 128:256] = lo
            hi, lo = two_terms(w.T)
            wtcat[0:128, rows] = hi
            wtcat[128:256, rows] = lo

    def ratio_block(rows):
        both = dot(wcat[rows, :], hcat[...])
        ratio = v_ref[rows, :] / (both[:, 0:128] + both[:, 128:256])
        hi, lo = two_terms(ratio)
        return jnp.concatenate([hi, lo], axis=1)

    def starts_of(half, size):
        return [pl.multiple_of(half * 512 + i, size) for i in range(0, 512, size)]

    def products(bases):
        acc = None
        for base in bases:
            rows = pl.ds(base, CHUNK)
            one = dot(wtcat[:, rows], ratio_block(rows))
            acc = one if acc is None else acc + one
        return acc

    def local_numer():
        return products(range(0, 1024, CHUNK))

    def joined(acc):
        low = acc[128:256, 0:128] + acc[0:128, 128:256] + acc[128:256, 128:256]
        return acc[0:128, 0:128] + low

    mine = (x, y)
    ring = (along_x, along_y)

    def rows_of(p, new_w):
        return PIECE + EXTRA if p == 0 and new_w else PIECE

    def copies(slot, phase, p, new_w):
        axis = (p + phase) % 2
        me = mine[axis]
        out, into = [], []
        for d in (2, 1, 3):
            for at, got in ((me, out), ((me + d) % 4, into)):
                block = xb.at[slot, phase, p, at, pl.ds(0, rows_of(p, new_w))]
                got.append(
                    pltpu.make_async_remote_copy(
                        src_ref=block,
                        dst_ref=block,
                        send_sem=x_send.at[slot, phase, p, d - 1],
                        recv_sem=x_recv.at[slot, phase, p, at],
                        device_id=ring[axis](d),
                        device_id_type=MESH,
                    )
                )
        return me, out, into

    def total_of(slot, phase, p, new_w):
        parts = [xb[slot, phase, p, i, 0 : rows_of(p, new_w)] for i in range(4)]
        return (parts[0] + parts[1]) + (parts[2] + parts[3])

    def nothing():
        pass

    def update_h(slot, numer=local_numer, new_w=False, first=nothing, second=nothing, third=nothing):
        new = joined(numer())
        plans = [[copies(slot, phase, p, new_w) for p in range(PIECES)] for phase in (0, 1)]
        for p in range(PIECES):
            xb[slot, 0, p, mine[p % 2], 0:PIECE] = new[p * PIECE : (p + 1) * PIECE]
        if new_w:
            xb[slot, 0, 0, x, PIECE : PIECE + EXTRA] = cpart[...]
        first()
        for _, out, _ in plans[0]:
            for c in out:
                c.start()
        settle()
        for p in range(PIECES):
            for c in plans[0][p][2]:
                c.wait_recv()
            me, out, _ = plans[1][p]
            xb[slot, 1, p, me, 0 : rows_of(p, new_w)] = total_of(slot, 0, p, new_w)
            for c in out:
                c.start()
        second()
        for _, out, _ in plans[0]:
            for c in out:
                c.wait_send()
        for p in range(PIECES):
            for c in plans[1][p][2]:
                c.wait_recv()
            full = total_of(slot, 1, p, new_w)
            if p == 0 and new_w:
                colsum = jnp.sum(full[PIECE:], axis=0, keepdims=True)
                inverse[...] = 1.0 / jnp.broadcast_to(colsum, (128, 128)).T
                full = full[0:PIECE]
            rows = slice(p * PIECE, (p + 1) * PIECE)
            fresh = h_ref[rows] * full * inverse[rows]
            h_ref[rows] = fresh
            hi, lo = two_terms(fresh)
            for base in (0, 128):
                again = slice(base + p * PIECE, base + (p + 1) * PIECE)
                hcat[again, 0:128] = hi
                hcat[again, 128:256] = lo
        third()
        for _, out, _ in plans[1]:
            pending.extend(out)

    def remote(src, dst, send, recv, to):
        return pltpu.make_async_remote_copy(
            src_ref=src, dst_ref=dst, send_sem=send, recv_sem=recv, device_id=to, device_id_type=MESH
        )

    def window(q):
        return (4 - 8 * ((q + core) % 2), 3, -3, 2, -2, 1, -1)

    def span(q):
        return pl.ds(0, PART + EXTRA) if q == 0 else pl.ds(EXTRA, PART)

    def update_w():
        turned = h_ref[...].T
        weights = twice(turned)
        rowsum = folded(turned)
        nsum[...] = rowsum

        def numer_of(half, b):
            rows = pl.ds(pl.multiple_of(half * 512 + b * CHUNK, CHUNK), CHUNK)
            both = dot(ratio_block(rows), weights)
            both = both[:, 0:128] + both[:, 128:256]
            for i in range(CHUNK // PART):
                place = b * (CHUNK // HALF) + i // PARTS
                nw[half, i % PARTS, place] = both[i * PART : (i + 1) * PART]

        def swap(q, step):
            way = group + q + step + core
            to = along_z(8 - 16 * (way % 2))
            return remote(
                tot.at[q, 2 * step, span(q)],
                tot.at[q, 2 * step + 1, span(q)],
                s_send.at[q, step],
                s_recv.at[q, step],
                to,
            )

        blocks = 512 // CHUNK
        each = 8 // blocks
        sums = remote(nsum, psum, p_send.at[PARTS * blocks], p_recv.at[PARTS * blocks], partner)
        sums.start()
        give = []
        for b in range(blocks):
            numer_of(other, b)
            for q in range(PARTS):
                at = pl.ds(b * each, each)
                i = b * PARTS + q
                c = remote(nw.at[other, q, at], pair.at[q, at], p_send.at[i], p_recv.at[i], partner)
                c.start()
                give.append(c)
        settle()
        for b in range(blocks):
            numer_of(core, b)
        sums.wait_recv()
        scatter, share, spread, over = [], [], [], []
        for q in range(PARTS):
            for b in range(blocks):
                give[b * PARTS + q].wait_recv()
            for k in range(8):
                if q == 0:
                    red[q, k, 0:EXTRA] = rowsum + psum[...]
                red[q, k, EXTRA : EXTRA + PART] = nw[core, q, k] + pair[q, k]
            moves = []
            for i, d in enumerate(window(q)):
                moves.append(
                    remote(
                        red.at[q, (kind + d + 8) % 8, span(q)],
                        win.at[q, i, span(q)],
                        n_send.at[q, i],
                        n_recv.at[q, i],
                        along_z(d),
                    )
                )
            for c in moves:
                c.start()
            scatter.append(moves)
        for q in range(PARTS):
            for c in scatter[q]:
                c.wait_recv()
            acc = red[q, kind, span(q)]
            for i in range(7):
                acc += win[q, i, span(q)]
            tot[q, 0, span(q)] = acc
            share.append([swap(q, 0)])
            share[q][0].start()
        for q in range(PARTS):
            share[q][0].wait_recv()
            tot[q, 2, span(q)] = tot[q, 0, span(q)] + tot[q, 1, span(q)]
            share[q].append(swap(q, 1))
            share[q][1].start()

        def part(q, which, owner):
            base = which * 512 + owner * HALF + q * PART
            return w_new.at[pl.ds(pl.multiple_of(base, PART), PART), :]

        below = None
        for q in range(PARTS):
            share[q][1].wait_recv()
            full = tot[q, 2, span(q)] + tot[q, 3, span(q)]
            if q == 0:
                below = jnp.sum(full[0:EXTRA], axis=0, keepdims=True)
                full = full[EXTRA : EXTRA + PART]
            here = pl.ds(pl.multiple_of(core * 512 + kind * HALF + q * PART, PART), PART)
            w_new[here, :] = w_in[here, :] * full / below
            block = part(q, core, kind)
            moves = []
            for i, d in enumerate(window(q)):
                moves.append(remote(block, block, g_send.at[q, i], g_recv.at[q, i], along_z(d)))
            for c in moves:
                c.start()
            spread.append(moves)
            c = remote(block, block, q_send.at[q, 7], q_recv.at[q, 7], partner)
            c.start()
            over.append(c)
        for q in range(PARTS):
            for i in (5, 6, 3, 4, 1, 2, 0):
                spread[q][i].wait_recv()
                block = part(q, core, (kind - window(q)[i] + 8) % 8)
                c = remote(block, block, q_send.at[q, i], q_recv.at[q, i], partner)
                c.start()
                over.append(c)
        pending.append(sums)
        for moves in scatter + share + spread + [give, over]:
            pending.extend(moves)

        def numer():
            take_w(w_new, starts_of(core, 128))
            acc = products(starts_of(core, CHUNK))
            for c in over:
                c.wait_recv()
            w_store.start()
            take_w(w_new, starts_of(other, 128))
            cpart[...] = folded(w_new[...])
            return acc + products(starts_of(other, CHUNK))

        return numer

    def enter():
        pl.semaphore_wait(barrier, len(near))
        tell(0)

    def step(i):
        def then():
            hear(i)
            if i < 2:
                tell(i + 1)

        return then

    w_store = pltpu.make_async_copy(w_new, w_out, out_sem)
    w_load.wait()
    take_w(w_in, range(0, 1024, 128))
    cpart[...] = folded(w_in[...])
    h_load.wait()
    hcat[...] = twice(h_ref[...])
    v_load.wait()
    update_h(0, local_numer, True, enter, step(0), step(1))
    update_h(1, second=step(2))
    update_h(0)
    numer = update_w()
    update_h(1, numer, True)
    update_h(0)
    h_out[...] = h_ref[...]
    settle()
    w_store.wait()


def pass_on(w, h, w_hbm_out, h_hbm_out, store):
    outs = [pltpu.make_async_copy(h, h_hbm_out, store.at[4])]
    for i in range(4):
        rows = pl.ds(i * 256, 256)
        outs.append(pltpu.make_async_copy(w.at[rows], w_hbm_out.at[rows], store.at[i]))
    for c in outs:
        c.start()
    for c in outs:
        c.wait()


def per_device(spectra, factor_w, factor_h):
    vmem = pl.BlockSpec(memory_space=pltpu.VMEM)
    hbm = pl.BlockSpec(memory_space=pl.ANY)
    dma = pltpu.SemaphoreType.DMA
    shapes = (jax.ShapeDtypeStruct((1024, 128), F32), jax.ShapeDtypeStruct((128, 128), F32))
    room = PART + EXTRA
    w, h = pl.pallas_call(
        kernel,
        out_shape=shapes,
        in_specs=[pl.BlockSpec(memory_space=pltpu.HBM)] * 3,
        out_specs=(vmem, vmem),
        scratch_shapes=[
            pltpu.VMEM((1024, 128), F32),
            pltpu.VMEM((1024, 128), F32),
            pltpu.VMEM((1024, 128), F32),
            dma((3,)),
            dma,
            pltpu.VMEM((128, 128), F32),
            pltpu.VMEM((1024, 256), BF16),
            pltpu.VMEM((256, 1024), BF16),
            pltpu.VMEM((256, 256), BF16),
            pltpu.VMEM((EXTRA, 128), F32),
            pltpu.VMEM((128, 128), F32),
            pltpu.VMEM((2, 2, PIECES, 4, PIECE + EXTRA, 128), F32),
            dma((2, 2, PIECES, 3)),
            dma((2, 2, PIECES, 4)),
            pltpu.SemaphoreType.REGULAR((3,)),
            pltpu.VMEM((2, PARTS, 8, PART, 128), F32),
            pltpu.VMEM((EXTRA, 128), F32),
            pltpu.VMEM((PARTS, 8, PART, 128), F32),
            pltpu.VMEM((EXTRA, 128), F32),
            pltpu.VMEM((PARTS, 8, room, 128), F32),
            pltpu.VMEM((PARTS, 7, room, 128), F32),
            pltpu.VMEM((PARTS, 4, room, 128), F32),
            dma((PARTS * 512 // CHUNK + 1,)), dma((PARTS * 512 // CHUNK + 1,)),
            dma((PARTS, 7)), dma((PARTS, 7)),
            dma((PARTS, 2)), dma((PARTS, 2)),
            dma((PARTS, 7)), dma((PARTS, 7)),
            dma((PARTS, 8)), dma((PARTS, 8)),
        ],
        compiler_params=pltpu.CompilerParams(
            collective_id=0, has_side_effects=True, vmem_limit_bytes=16 * 2**20
        ),
        name="nmf",
    )(*(pltpu.with_memory_space_constraint(a, pltpu.HBM) for a in (spectra, factor_w, factor_h)))
    return pl.pallas_call(
        pass_on,
        out_shape=shapes,
        in_specs=[vmem, vmem],
        out_specs=(hbm, hbm),
        scratch_shapes=[dma((5,))],
        compiler_params=pltpu.CompilerParams(vmem_limit_bytes=8 * 2**20),
        name="pass_on",
    )(w, h)


def solution(mesh):
    return jax.shard_map(
        per_device,
        mesh=mesh,
        in_specs=(P("row", "col"), P("row", None), P(None, "col")),
        out_specs=(P("row", None), P(None, "col")),
        check_vma=False,
    )
```
